32 devices in a mesh: db: 8 (over y, x, core), pb: 4 (over z).
Axes of the slice: x: 2, y: 2, z: 4, core: 2. Of those that a mesh axis runs over, the one named last changes fastest.
Arguments:
- query_maps: bfloat16 [32, 256, 256], P(('db', 'pb')), may hold values from -6 to 6
- database: bfloat16 [1024, 256, 256], P(('db', 'pb')), may hold values from -6 to 6
- shortlist: int32 [32, 128], P(('db', 'pb')), may hold values from 0 to 1023, as said below
- kernel_query: bfloat16 [3, 3], replicated, may hold values from -1.5 to 1.5
- kernel_db: bfloat16 [3, 3], replicated, may hold values from -1.5 to 1.5
Outputs:
- scores: float32 [32, 128], P(('db', 'pb'))
- top_scores: float32 [32, 100], P(('db', 'pb'))
The draws below stay inside these ranges and needn't reach their ends.
Inputs may be any that keep to these rules, and one draw needn't show every extreme that they name: Within one query the ids are distinct. Among the 128 shortlist entries of the query held by device q (query q), at most 8 lie in any one shard of images (ids s * 32 to (s + 1) * 32 - 1), and some shard holds exactly 8 of them for every device.
All inputs are finite; a program needn't handle non-finite values.
Results may differ from the reference program's by a relative error of at most 0.0003.
Values may be sent and summed in bfloat16 or wider, within the bound.
A program may use at most 128 MiB of HBM per device.

```python
import jax
import jax.numpy as jnp
from jax import lax

C = 256
GRID = 16
CAND = 128
TOPK = 100
Q_DEV = 1
IMG_DEV = 32
NQ = 32
DB_IMG = 1024
CAP = 8


def draw_shortlist(key, part):
    shard_count = DB_IMG // IMG_DEV
    block_count = NQ // Q_DEV
    entry_count = shard_count * CAP
    take_count = Q_DEV * CAND
    hottest = jax.random.randint(jax.random.fold_in(key, 11), (), 0, shard_count)

    def one_slots(slot_key):
        return jax.random.permutation(slot_key, IMG_DEV)[:CAP]

    def one_block(block_key):
        first_key, second_key, third_key = jax.random.split(block_key, 3)
        order = jax.random.permutation(first_key, entry_count)
        shard_entry = jnp.arange(entry_count) // CAP
        priority = order + jnp.where(shard_entry == hottest, -entry_count, 0)
        chosen = jnp.argsort(priority)[:take_count]
        chosen = chosen[jax.random.permutation(second_key, take_count)]
        shard_pick = chosen // CAP
        within = chosen % CAP
        slot_table = jax.vmap(one_slots)(jax.random.split(third_key, shard_count))
        image_ids = shard_pick * IMG_DEV + slot_table[shard_pick, within]
        return image_ids.reshape(Q_DEV, CAND)
    block_keys = jax.random.split(jax.random.fold_in(key, 12), block_count)
    return jax.vmap(one_block)(block_keys).reshape(NQ, CAND).astype(jnp.int32)


def levels(key, shape, shards, smallest, high):
    factor_of = 1.0
    for position, blocks in shards:
        heights = jax.random.uniform(jax.random.fold_in(jax.random.fold_in(key, 6), position), (blocks,), jnp.float32, smallest / len(shards), high / len(shards))
        factor_of = factor_of * jnp.repeat(jnp.exp(heights), shape[position] // blocks).reshape((-1,) + (1,) * (len(shape) - 1 - position))
    return factor_of


def bell_draw(key, dims, spread, reach, cuts=(), kind=jnp.bfloat16):
    array = jax.random.normal(key, dims, jnp.float32) * spread
    if len(cuts) > 0:
        array = levels(key, dims, cuts, -0.22, 0.18) * array
    return jnp.clip(array, min=-reach, max=reach).astype(kind)


def setup_inputs(seed: int = 0) -> dict:
    streams_of = jax.random.split(jax.random.key(seed), 6)
    query_maps = bell_draw(streams_of[0], (NQ, C, GRID * GRID), 1.0, 6.0, ((0, 32),))
    database = bell_draw(streams_of[1], (DB_IMG, C, GRID * GRID), 1.0, 6.0, ((0, 32),))
    shortlist = draw_shortlist(jax.random.fold_in(streams_of[5], 71), 0)
    kernel_query = bell_draw(streams_of[3], (3, 3), 0.33, 1.5)
    kernel_db = bell_draw(streams_of[4], (3, 3), 0.33, 1.5)
    return {"query_maps": query_maps, "database": database, "shortlist": shortlist, "kernel_query": kernel_query, "kernel_db": kernel_db}


epsilon = 1e-06
score_scale = 8.0

def unit_maps(maps):
    values = maps.astype(jnp.float32)
    squares = lax.optimization_barrier(jnp.sum(values * values, axis=1, keepdims=True))
    return (values * lax.rsqrt(squares + epsilon)).astype(jnp.bfloat16)

def reference(query_maps, database, shortlist, kernel_query, kernel_db):
    query_unit = unit_maps(query_maps)
    taps_query = kernel_query.astype(jnp.float32)
    taps_db = kernel_db.astype(jnp.float32)

    def per_query(inputs):
        query_one, image_ids = inputs
        images = unit_maps(database[image_ids.astype(jnp.int32)])
        correlation = jnp.einsum('cq,ncd->nqd', query_one.astype(jnp.float32), images.astype(jnp.float32))
        rectified = jnp.maximum(correlation, 0.0).astype(jnp.bfloat16)
        rectified = lax.optimization_barrier(rectified).astype(jnp.float32)
        grid_form = rectified.reshape(CAND, GRID, GRID, GRID, GRID)
        pad_query = jnp.pad(grid_form, ((0, 0), (1, 1), (1, 1), (0, 0), (0, 0)))
        pad_db = jnp.pad(grid_form, ((0, 0), (0, 0), (0, 0), (1, 1), (1, 1)))
        filtered = jnp.zeros_like(grid_form)
        for i in range(3):
            for j in range(3):
                filtered = filtered + taps_query[i, j] * pad_query[:, i:i + GRID, j:j + GRID, :, :]
                filtered = filtered + taps_db[i, j] * pad_db[:, :, :, i:i + GRID, j:j + GRID]
        filtered = filtered.reshape(CAND, GRID * GRID, GRID * GRID)
        return score_scale * lax.optimization_barrier(jnp.mean(lax.optimization_barrier(jnp.max(filtered, axis=1)), axis=-1))
    scores = lax.map(per_query, (query_unit, shortlist))
    top_scores = lax.top_k(scores, TOPK)[0]
    return (scores, top_scores)
```

```python
import functools

import jax
import jax.numpy as jnp
from jax import lax
from jax.experimental import pallas as pl
from jax.experimental.pallas import tpu as pltpu
from jax.sharding import PartitionSpec as P

GRID = 16
TOPK = 100
LANES = 128
ROWS = 8
MESH = pl.DeviceIdType.MESH

epsilon = 1e-06
score_scale = 8.0


def unit_maps(maps):
    values = maps.astype(jnp.float32)
    squares = jnp.sum(values * values, axis=1, keepdims=True)
    return (values * lax.rsqrt(squares + epsilon)).astype(jnp.bfloat16)


def conv_matrix(kernel):
    cell_count = GRID * GRID
    cell_index = jnp.arange(cell_count)
    row_out = (cell_index // GRID)[:, None]
    col_out = (cell_index % GRID)[:, None]
    row_in = (cell_index // GRID)[None, :]
    col_in = (cell_index % GRID)[None, :]
    weights = kernel.astype(jnp.float32)
    matrix = jnp.zeros((cell_count, cell_count), jnp.float32)
    for i in range(3):
        for j in range(3):
            hit = (row_in == row_out + i - 1) & (col_in == col_out + j - 1)
            matrix = matrix + weights[i, j] * hit.astype(jnp.float32)
    return matrix.astype(jnp.bfloat16)


def kernel(
    db_count,
    pb_count,
    width,
    query_ref,
    info_ref,
    database_ref,
    conv_query_ref,
    conv_db_ref,
    out_ref,
    maps,
    infos,
    units,
    slot_rows,
    slot_table,
    peaks,
    found,
    returned,
    map_send,
    map_recv,
    info_send,
    info_recv,
    back_send,
    back_recv,
    local_sem,
):
    count = db_count * pb_count
    chips = db_count // 2
    image_count = database_ref.shape[0]
    db = lax.axis_index("db")
    pb = lax.axis_index("pb")
    chip = db // 2
    core = lax.rem(db, 2)
    me = db * pb_count + pb

    def place(index):
        return (index // pb_count, lax.rem(index, pb_count))

    def index_of(other_pb, other_chip, other_core):
        return (other_chip * 2 + other_core) * pb_count + other_pb

    def map_copy(source, block, send_slot, device):
        return pltpu.make_async_remote_copy(
            src_ref=block,
            dst_ref=maps.at[source],
            send_sem=map_send.at[send_slot],
            recv_sem=map_recv.at[source],
            device_id=device,
            device_id_type=MESH,
        )

    def info_copy(other, owner):
        return pltpu.make_async_remote_copy(
            src_ref=info_ref,
            dst_ref=infos.at[owner],
            send_sem=info_send.at[other],
            recv_sem=info_recv.at[owner],
            device_id=place(other),
            device_id_type=MESH,
        )

    def back_copy(source, landed):
        return pltpu.make_async_remote_copy(
            src_ref=found.at[source],
            dst_ref=returned.at[landed],
            send_sem=back_send.at[source],
            recv_sem=back_recv.at[landed],
            device_id=place(source),
            device_id_type=MESH,
        )

    barrier = pltpu.get_barrier_semaphore()

    @pl.loop(1, count)
    def _(step):
        pl.semaphore_signal(
            barrier, inc=1, device_id=place(lax.rem(me + step, count)), device_id_type=MESH
        )

    pl.semaphore_wait(barrier, count - 1)

    plane_base = pb_count
    partner_base = pb_count + pb_count * chips

    for step in range(1, pb_count):
        map_copy(me, query_ref, step, (db, lax.rem(pb + step, pb_count))).start()
    for step in range(1, chips):
        map_copy(
            me, query_ref, plane_base + step, (lax.rem(chip + step, chips) * 2 + core, pb)
        ).start()

    @pl.loop(1, count)
    def _(step):
        info_copy(lax.rem(me + step, count), me).start()

    map_copy(me, query_ref, partner_base, (chip * 2 + 1 - core, pb)).start()
    maps[me] = query_ref[...]
    infos[me] = info_ref[...]

    @pl.loop(0, image_count)
    def _(image):
        values = database_ref[image].astype(jnp.float32)
        squares = jnp.sum(values * values, axis=0, keepdims=True)
        units[image] = (values * lax.rsqrt(squares + epsilon)).astype(jnp.bfloat16)

    @pl.loop(1, count)
    def _(step):
        info_copy(lax.rem(me + step, count), lax.rem(me + step, count)).wait_recv()

    shard_of = infos[:, 0, :]
    slot_of = infos[:, 1, :]
    bucket_of = infos[:, 2, :]
    lane = lax.broadcasted_iota(jnp.int32, (count, LANES), 1)
    table = jnp.zeros((count, LANES), jnp.int32)
    for k in range(width):
        hit = (shard_of == me) & (bucket_of == k)
        slot = jnp.sum(jnp.where(hit, slot_of, 0), axis=1, keepdims=True)
        table = jnp.where(lane == k, slot, table)
    slot_rows[...] = table
    to_smem = pltpu.make_async_copy(slot_rows, slot_table, local_sem)
    to_smem.start()
    to_smem.wait()
    peaks[...] = jnp.zeros_like(peaks)

    @pl.loop(0, count)
    def _(turn):
        step = turn // 2
        half = lax.rem(turn, 2)
        hop = lax.rem(step, chips)
        other_pb = lax.rem(pb + step // chips, pb_count)
        other_chip = lax.rem(chip + hop, chips)
        source = index_of(other_pb, other_chip, lax.rem(core + half, 2))

        @pl.when((half == 0) & (step >= 1) & (step < pb_count))
        def _():
            line_pb = lax.rem(pb + step, pb_count)
            line = index_of(line_pb, chip, core)
            map_copy(line, maps.at[line], 0, (db, line_pb)).wait_recv()
            for d in range(1, chips):
                map_copy(
                    line,
                    maps.at[line],
                    plane_base + step * chips + d,
                    (lax.rem(chip + d, chips) * 2 + core, pb),
                ).start()

        @pl.when((half == 1) | (hop != 0))
        def _():
            map_copy(source, maps.at[source], 0, (chip * 2 + 1 - core, pb)).wait_recv()

        @pl.when((half == 0) & (step != 0))
        def _():
            map_copy(
                source, maps.at[source], partner_base + step, (chip * 2 + 1 - core, pb)
            ).start()

        for k in range(width):
            slot = slot_table[source, k]
            correlation = jnp.dot(
                maps[source], units[slot], preferred_element_type=jnp.float32
            )
            rectified = jnp.maximum(correlation, 0.0).astype(jnp.bfloat16)
            filtered = jnp.dot(
                conv_query_ref[...], rectified, preferred_element_type=jnp.float32
            ) + jnp.dot(rectified, conv_db_ref[...], preferred_element_type=jnp.float32)
            peaks[k : k + 1, :] = jnp.max(filtered, axis=0, keepdims=True)
        best = peaks[...]
        total = jnp.sum(best, axis=1, keepdims=True) * (score_scale / best.shape[1])
        found[source] = jnp.broadcast_to(total, (ROWS, LANES))

        @pl.when(source != me)
        def _():
            back_copy(source, me).start()

    returned[me] = found[me]

    @pl.loop(1, count)
    def _(step):
        other = lax.rem(me + step, count)
        back_copy(other, other).wait_recv()

    my_shard = info_ref[0:1, :]
    my_bucket = info_ref[2:3, :]
    rank = lax.broadcasted_iota(jnp.int32, (ROWS, LANES), 0)
    scores = jnp.zeros((ROWS, LANES), jnp.float32)
    for s in range(count):
        scores = scores + jnp.where((my_shard == s) & (my_bucket == rank), returned[s], 0.0)
    out_ref[...] = jnp.sum(scores, axis=0, keepdims=True)

    @pl.loop(1, count)
    def _(step):
        other = lax.rem(me + step, count)
        info_copy(other, me).wait_send()
        back_copy(other, me).wait_send()

    for step in range(1, pb_count):
        map_copy(me, query_ref, step, (db, pb)).wait_send()
    for step in range(pb_count):
        for d in range(1, chips):
            map_copy(me, query_ref, plane_base + step * chips + d, (db, pb)).wait_send()

    @pl.loop(0, pb_count * chips)
    def _(step):
        map_copy(me, query_ref, partner_base + step, (db, pb)).wait_send()


def body(db_count, pb_count, query_maps, database, shortlist, kernel_query, kernel_db):
    count = db_count * pb_count
    chips = db_count // 2
    image_count, channels, cells = database.shape
    entries = shortlist.shape[1]
    width = 2 * entries // count
    query_unit = jnp.swapaxes(unit_maps(query_maps)[0], 0, 1)
    conv_query = conv_matrix(kernel_query)
    conv_db = conv_matrix(kernel_db).T
    ids = shortlist[0]
    shard_of = ids // image_count
    slot_of = ids % image_count
    order = jnp.arange(entries, dtype=jnp.int32)
    earlier = (shard_of[:, None] == shard_of[None, :]) & (order[:, None] < order[None, :])
    bucket_of = jnp.sum(earlier.astype(jnp.int32), axis=0)
    unused = jnp.zeros((ROWS - 3, entries), jnp.int32)
    info = jnp.concatenate([jnp.stack([shard_of, slot_of, bucket_of]), unused])
    vmem = pl.BlockSpec(memory_space=pltpu.VMEM)
    scores = pl.pallas_call(
        functools.partial(kernel, db_count, pb_count, width),
        out_shape=jax.ShapeDtypeStruct((1, entries), jnp.float32),
        in_specs=[vmem] * 5,
        out_specs=vmem,
        scratch_shapes=[
            pltpu.VMEM((count, cells, channels), jnp.bfloat16),
            pltpu.VMEM((count, ROWS, LANES), jnp.int32),
            pltpu.VMEM((image_count, channels, cells), jnp.bfloat16),
            pltpu.VMEM((count, LANES), jnp.int32),
            pltpu.SMEM((count, LANES), jnp.int32),
            pltpu.VMEM((ROWS, cells), jnp.float32),
            pltpu.VMEM((count, ROWS, LANES), jnp.float32),
            pltpu.VMEM((count, ROWS, LANES), jnp.float32),
            pltpu.SemaphoreType.DMA((pb_count + 2 * pb_count * chips,)),
            pltpu.SemaphoreType.DMA((count,)),
            pltpu.SemaphoreType.DMA((count,)),
            pltpu.SemaphoreType.DMA((count,)),
            pltpu.SemaphoreType.DMA((count,)),
            pltpu.SemaphoreType.DMA((count,)),
            pltpu.SemaphoreType.DMA,
        ],
        compiler_params=pltpu.CompilerParams(
            collective_id=0, has_side_effects=True, vmem_limit_bytes=56 * 1024 * 1024
        ),
    )(query_unit, info, database, conv_query, conv_db)
    return (scores, lax.top_k(scores, TOPK)[0])


def solution(mesh):
    in_specs = (
        P(("db", "pb"), None, None),
        P(("db", "pb"), None, None),
        P(("db", "pb"), None),
        P(),
        P(),
    )
    out_specs = (P(("db", "pb"), None), P(("db", "pb"), None))
    step = functools.partial(body, mesh.shape["db"], mesh.shape["pb"])
    return jax.shard_map(step, mesh=mesh, in_specs=in_specs, out_specs=out_specs, check_vma=False)
```

```python
import functools

import jax
import jax.numpy as jnp
from jax import lax
from jax.experimental import pallas as pl
from jax.experimental.pallas import tpu as pltpu
from jax.sharding import PartitionSpec as P

GRID = 16
TOPK = 100
LANES = 128
ROWS = 8
MESH = pl.DeviceIdType.MESH

epsilon = 1e-06
score_scale = 8.0


def unit_map(values):
    squares = jnp.sum(values * values, axis=0, keepdims=True)
    return values * lax.rsqrt(squares + epsilon)


def fill_filters(query_taps, db_taps, filter_query, filter_db):
    cells = filter_query.shape[0]
    row = lax.broadcasted_iota(jnp.int32, (cells, cells), 0)
    col = lax.broadcasted_iota(jnp.int32, (cells, cells), 1)
    down = (col >> 4) - (row >> 4)
    across = (col & (GRID - 1)) - (row & (GRID - 1))
    near = (jnp.abs(down) <= 1) & (jnp.abs(across) <= 1)
    tap = jnp.where(near, down * 3 + across + 4, -1)
    query_matrix = jnp.zeros((cells, cells), jnp.float32)
    db_matrix = jnp.zeros((cells, cells), jnp.float32)
    query_values = query_taps[...].astype(jnp.float32)
    db_values = db_taps[...].astype(jnp.float32)
    for i in range(3):
        for j in range(3):
            hit = tap == 3 * i + j
            back = tap == 8 - (3 * i + j)
            query_matrix = jnp.where(hit, query_values[i : i + 1, j : j + 1], query_matrix)
            db_matrix = jnp.where(back, db_values[i : i + 1, j : j + 1], db_matrix)
    filter_query[...] = query_matrix.astype(jnp.bfloat16)
    filter_db[...] = db_matrix.astype(jnp.bfloat16)


def descending(row):
    entries = row.shape[1]
    across = jnp.broadcast_to(row, (entries, entries))
    down = across.T
    above = lax.broadcasted_iota(jnp.int32, (entries, entries), 0)
    beside = lax.broadcasted_iota(jnp.int32, (entries, entries), 1)
    ahead = (down > across) | ((down == across) & (above < beside))
    rank = jnp.sum(jnp.where(ahead, 1.0, 0.0), axis=0, keepdims=True)
    rank_down = jnp.broadcast_to(rank, (entries, entries)).T
    chosen = jnp.where(rank_down == beside.astype(jnp.float32), down, 0.0)
    return jnp.sum(chosen, axis=0, keepdims=True)


def kernel(
    db_count,
    pb_count,
    width,
    query_ref,
    info_ref,
    database_ref,
    query_taps,
    db_taps,
    out_ref,
    sorted_ref,
    filter_query,
    filter_db,
    raw,
    positive,
    maps,
    infos,
    units,
    slot_rows,
    slot_table,
    peaks,
    found,
    returned,
    map_send,
    map_recv,
    info_send,
    info_recv,
    back_send,
    back_recv,
    local_sem,
    raw_sem,
):
    count = db_count * pb_count
    chips = db_count // 2
    image_count = database_ref.shape[0]
    db = lax.axis_index("db")
    pb = lax.axis_index("pb")
    chip = db // 2
    core = lax.rem(db, 2)
    me = db * pb_count + pb

    def place(index):
        return (index // pb_count, lax.rem(index, pb_count))

    def index_of(other_pb, other_chip, other_core):
        return (other_chip * 2 + other_core) * pb_count + other_pb

    def map_copy(source, block, send_slot, device):
        return pltpu.make_async_remote_copy(
            src_ref=block,
            dst_ref=maps.at[source],
            send_sem=map_send.at[send_slot],
            recv_sem=map_recv.at[source],
            device_id=device,
            device_id_type=MESH,
        )

    def info_copy(other, owner):
        return pltpu.make_async_remote_copy(
            src_ref=info_ref,
            dst_ref=infos.at[owner],
            send_sem=info_send.at[other],
            recv_sem=info_recv.at[owner],
            device_id=place(other),
            device_id_type=MESH,
        )

    def back_copy(source, landed):
        return pltpu.make_async_remote_copy(
            src_ref=found.at[source],
            dst_ref=returned.at[landed],
            send_sem=back_send.at[source],
            recv_sem=back_recv.at[landed],
            device_id=place(source),
            device_id_type=MESH,
        )

    def raw_copy(image):
        return pltpu.make_async_copy(database_ref.at[image], raw.at[image], raw_sem.at[image])

    barrier = pltpu.get_barrier_semaphore()

    @pl.loop(1, count)
    def _(step):
        pl.semaphore_signal(
            barrier, inc=1, device_id=place(lax.rem(me + step, count)), device_id_type=MESH
        )

    @pl.loop(0, image_count)
    def _(image):
        raw_copy(image).start()

    maps[me] = unit_map(query_ref[0].astype(jnp.float32)).T.astype(jnp.bfloat16)
    infos[me] = info_ref[...]
    fill_filters(query_taps, db_taps, filter_query, filter_db)
    pl.semaphore_wait(barrier, count - 1)

    plane_base = pb_count
    partner_base = pb_count + pb_count * chips

    for step in range(1, pb_count):
        map_copy(me, maps.at[me], step, (db, lax.rem(pb + step, pb_count))).start()
    for step in range(1, chips):
        map_copy(
            me, maps.at[me], plane_base + step, (lax.rem(chip + step, chips) * 2 + core, pb)
        ).start()

    @pl.loop(1, count)
    def _(step):
        info_copy(lax.rem(me + step, count), me).start()

    map_copy(me, maps.at[me], partner_base, (chip * 2 + 1 - core, pb)).start()

    @pl.loop(0, image_count)
    def _(image):
        raw_copy(image).wait()
        units[image] = unit_map(raw[image].astype(jnp.float32)).astype(jnp.bfloat16)

    @pl.loop(1, count)
    def _(step):
        info_copy(lax.rem(me + step, count), lax.rem(me + step, count)).wait_recv()

    shard_of = infos[:, 0, :]
    slot_of = infos[:, 1, :]
    bucket_of = infos[:, 2, :]
    lane = lax.broadcasted_iota(jnp.int32, (count, LANES), 1)
    table = jnp.zeros((count, LANES), jnp.int32)
    for k in range(width):
        hit = (shard_of == me) & (bucket_of == k)
        slot = jnp.sum(jnp.where(hit, slot_of, 0), axis=1, keepdims=True)
        table = jnp.where(lane == k, slot, table)
    slot_rows[...] = table
    to_smem = pltpu.make_async_copy(slot_rows, slot_table, local_sem)
    to_smem.start()
    to_smem.wait()
    peaks[...] = jnp.zeros_like(peaks)

    @pl.loop(0, count)
    def _(turn):
        step = turn // 2
        half = lax.rem(turn, 2)
        hop = lax.rem(step, chips)
        other_pb = lax.rem(pb + step // chips, pb_count)
        other_chip = lax.rem(chip + hop, chips)
        source = index_of(other_pb, other_chip, lax.rem(core + half, 2))

        @pl.when((half == 0) & (step >= 1) & (step < pb_count))
        def _():
            line_pb = lax.rem(pb + step, pb_count)
            line = index_of(line_pb, chip, core)
            map_copy(line, maps.at[line], 0, (db, line_pb)).wait_recv()
            for d in range(1, chips):
                map_copy(
                    line,
                    maps.at[line],
                    plane_base + step * chips + d,
                    (lax.rem(chip + d, chips) * 2 + core, pb),
                ).start()

        @pl.when((half == 1) | (hop != 0))
        def _():
            map_copy(source, maps.at[source], 0, (chip * 2 + 1 - core, pb)).wait_recv()

        @pl.when((half == 0) & (step != 0))
        def _():
            map_copy(
                source, maps.at[source], partner_base + step, (chip * 2 + 1 - core, pb)
            ).start()

        for k in range(width):
            slot = slot_table[source, k]
            correlation = jnp.dot(
                maps[source], units[slot], preferred_element_type=jnp.float32
            )
            positive[k] = jnp.maximum(correlation, 0.0).astype(jnp.bfloat16)
        for k in range(width):
            rectified = positive[k]
            filtered = jnp.dot(
                filter_query[...], rectified, preferred_element_type=jnp.float32
            ) + jnp.dot(rectified, filter_db[...], preferred_element_type=jnp.float32)
            peaks[k : k + 1, :] = jnp.max(filtered, axis=0, keepdims=True)
        best = peaks[...]
        total = jnp.sum(best, axis=1, keepdims=True) * (score_scale / best.shape[1])
        found[source] = jnp.broadcast_to(total, (ROWS, LANES))

        @pl.when(source != me)
        def _():
            back_copy(source, me).start()

    returned[me] = found[me]

    @pl.loop(1, count)
    def _(step):
        other = lax.rem(me + step, count)
        back_copy(other, other).wait_recv()

    my_shard = info_ref[0:1, :]
    my_bucket = info_ref[2:3, :]
    rank = lax.broadcasted_iota(jnp.int32, (ROWS, LANES), 0)
    scores = jnp.zeros((ROWS, LANES), jnp.float32)
    for s in range(count):
        scores = scores + jnp.where((my_shard == s) & (my_bucket == rank), returned[s], 0.0)
    final = jnp.sum(scores, axis=0, keepdims=True)
    out_ref[...] = final
    sorted_ref[...] = descending(final)

    @pl.loop(1, count)
    def _(step):
        other = lax.rem(me + step, count)
        info_copy(other, me).wait_send()
        back_copy(other, me).wait_send()

    for step in range(1, pb_count):
        map_copy(me, maps.at[me], step, (db, pb)).wait_send()
    for step in range(pb_count):
        for d in range(1, chips):
            map_copy(me, maps.at[me], plane_base + step * chips + d, (db, pb)).wait_send()

    @pl.loop(0, pb_count * chips)
    def _(step):
        map_copy(me, maps.at[me], partner_base + step, (db, pb)).wait_send()


def body(db_count, pb_count, query_maps, database, shortlist, kernel_query, kernel_db):
    count = db_count * pb_count
    chips = db_count // 2
    image_count, channels, cells = database.shape
    entries = shortlist.shape[1]
    width = 2 * entries // count
    ids = shortlist[0]
    shard_of = ids // image_count
    slot_of = ids % image_count
    order = jnp.arange(entries, dtype=jnp.int32)
    earlier = (shard_of[:, None] == shard_of[None, :]) & (order[:, None] < order[None, :])
    bucket_of = jnp.sum(earlier.astype(jnp.int32), axis=0)
    unused = jnp.zeros((ROWS - 3, entries), jnp.int32)
    info = jnp.concatenate([jnp.stack([shard_of, slot_of, bucket_of]), unused])
    vmem = pl.BlockSpec(memory_space=pltpu.VMEM)
    row = jax.ShapeDtypeStruct((1, entries), jnp.float32)
    scores, ordered = pl.pallas_call(
        functools.partial(kernel, db_count, pb_count, width),
        out_shape=(row, row),
        in_specs=[vmem, vmem, pl.BlockSpec(memory_space=pl.ANY), vmem, vmem],
        out_specs=(vmem, vmem),
        scratch_shapes=[
            pltpu.VMEM((cells, cells), jnp.bfloat16),
            pltpu.VMEM((cells, cells), jnp.bfloat16),
            pltpu.VMEM((image_count, channels, cells), jnp.bfloat16),
            pltpu.VMEM((width, cells, cells), jnp.bfloat16),
            pltpu.VMEM((count, cells, channels), jnp.bfloat16),
            pltpu.VMEM((count, ROWS, LANES), jnp.int32),
            pltpu.VMEM((image_count, channels, cells), jnp.bfloat16),
            pltpu.VMEM((count, LANES), jnp.int32),
            pltpu.SMEM((count, LANES), jnp.int32),
            pltpu.VMEM((ROWS, cells), jnp.float32),
            pltpu.VMEM((count, ROWS, LANES), jnp.float32),
            pltpu.VMEM((count, ROWS, LANES), jnp.float32),
            pltpu.SemaphoreType.DMA((pb_count + 2 * pb_count * chips,)),
            pltpu.SemaphoreType.DMA((count,)),
            pltpu.SemaphoreType.DMA((count,)),
            pltpu.SemaphoreType.DMA((count,)),
            pltpu.SemaphoreType.DMA((count,)),
            pltpu.SemaphoreType.DMA((count,)),
            pltpu.SemaphoreType.DMA,
            pltpu.SemaphoreType.DMA((image_count,)),
        ],
        compiler_params=pltpu.CompilerParams(
            collective_id=0, has_side_effects=True, vmem_limit_bytes=56 * 1024 * 1024
        ),
    )(query_maps, info, database, kernel_query, kernel_db)
    return (scores, ordered[:, :TOPK])


def solution(mesh):
    in_specs = (
        P(("db", "pb"), None, None),
        P(("db", "pb"), None, None),
        P(("db", "pb"), None),
        P(),
        P(),
    )
    out_specs = (P(("db", "pb"), None), P(("db", "pb"), None))
    step = functools.partial(body, mesh.shape["db"], mesh.shape["pb"])
    return jax.shard_map(step, mesh=mesh, in_specs=in_specs, out_specs=out_specs, check_vma=False)
```

```python
import functools

import jax
import jax.numpy as jnp
from jax import lax
from jax.experimental import pallas as pl
from jax.experimental.pallas import tpu as pltpu
from jax.sharding import PartitionSpec as P

GRID = 16
TOPK = 100
LANES = 128
ROWS = 8
MESH = pl.DeviceIdType.MESH

epsilon = 1e-06
score_scale = 8.0


def unit_map(values):
    squares = jnp.sum(values * values, axis=0, keepdims=True)
    return values * lax.rsqrt(squares + epsilon)


def fill_filters(query_taps, db_taps, filter_query, filter_db):
    cells = filter_query.shape[0]
    row = lax.broadcasted_iota(jnp.int32, (cells, cells), 0)
    col = lax.broadcasted_iota(jnp.int32, (cells, cells), 1)
    down = (col >> 4) - (row >> 4)
    across = (col & (GRID - 1)) - (row & (GRID - 1))
    near = (jnp.abs(down) <= 1) & (jnp.abs(across) <= 1)
    tap = jnp.where(near, down * 3 + across + 4, -1)
    query_matrix = jnp.zeros((cells, cells), jnp.float32)
    db_matrix = jnp.zeros((cells, cells), jnp.float32)
    query_values = query_taps[...].astype(jnp.float32)
    db_values = db_taps[...].astype(jnp.float32)
    for i in range(3):
        for j in range(3):
            hit = tap == 3 * i + j
            back = tap == 8 - (3 * i + j)
            query_matrix = jnp.where(hit, query_values[i : i + 1, j : j + 1], query_matrix)
            db_matrix = jnp.where(back, db_values[i : i + 1, j : j + 1], db_matrix)
    filter_query[...] = query_matrix.astype(jnp.bfloat16)
    filter_db[...] = db_matrix.astype(jnp.bfloat16)


def shortlist_info(ids, image_count, count):
    entries = ids.shape[1]
    shard = jnp.zeros_like(ids)
    for s in range(1, count):
        shard = shard + jnp.where(ids >= s * image_count, 1, 0)
    slot = ids - shard * image_count
    across = jnp.broadcast_to(shard, (entries, entries))
    above = lax.broadcasted_iota(jnp.int32, (entries, entries), 0)
    beside = lax.broadcasted_iota(jnp.int32, (entries, entries), 1)
    earlier = (across.T == across) & (above < beside)
    bucket = jnp.sum(jnp.where(earlier, 1, 0), axis=0, keepdims=True)
    rank = lax.broadcasted_iota(jnp.int32, (ROWS, entries), 0)
    return jnp.where(rank == 0, shard, jnp.where(rank == 1, slot, bucket))


def descending(row):
    entries = row.shape[1]
    across = jnp.broadcast_to(row, (entries, entries))
    down = across.T
    above = lax.broadcasted_iota(jnp.int32, (entries, entries), 0)
    beside = lax.broadcasted_iota(jnp.int32, (entries, entries), 1)
    ahead = (down > across) | ((down == across) & (above < beside))
    rank = jnp.sum(jnp.where(ahead, 1.0, 0.0), axis=0, keepdims=True)
    rank_down = jnp.broadcast_to(rank, (entries, entries)).T
    chosen = jnp.where(rank_down == beside.astype(jnp.float32), down, 0.0)
    return jnp.sum(chosen, axis=0, keepdims=True)


def kernel(
    db_count,
    pb_count,
    width,
    query_ref,
    shortlist_ref,
    database_ref,
    query_taps,
    db_taps,
    out_ref,
    sorted_ref,
    filter_query,
    filter_db,
    raw,
    positive,
    maps,
    infos,
    units,
    slot_rows,
    slot_table,
    own_rows,
    own_table,
    current,
    peaks,
    found,
    returned,
    map_send,
    map_recv,
    info_send,
    info_recv,
    back_send,
    back_recv,
    local_sem,
    own_sem,
    raw_sem,
):
    count = db_count * pb_count
    chips = db_count // 2
    image_count = database_ref.shape[0]
    db = lax.axis_index("db")
    pb = lax.axis_index("pb")
    chip = db // 2
    core = lax.rem(db, 2)
    me = db * pb_count + pb

    def place(index):
        return (index // pb_count, lax.rem(index, pb_count))

    def index_of(other_pb, other_chip, other_core):
        return (other_chip * 2 + other_core) * pb_count + other_pb

    def map_copy(source, block, send_slot, device):
        return pltpu.make_async_remote_copy(
            src_ref=block,
            dst_ref=maps.at[source],
            send_sem=map_send.at[send_slot],
            recv_sem=map_recv.at[source],
            device_id=device,
            device_id_type=MESH,
        )

    def info_copy(other, owner):
        return pltpu.make_async_remote_copy(
            src_ref=infos.at[me],
            dst_ref=infos.at[owner],
            send_sem=info_send.at[other],
            recv_sem=info_recv.at[owner],
            device_id=place(other),
            device_id_type=MESH,
        )

    def back_copy(source, landed):
        return pltpu.make_async_remote_copy(
            src_ref=found.at[source],
            dst_ref=returned.at[landed],
            send_sem=back_send.at[source],
            recv_sem=back_recv.at[landed],
            device_id=place(source),
            device_id_type=MESH,
        )

    def raw_copy(image):
        return pltpu.make_async_copy(database_ref.at[image], raw.at[image], raw_sem.at[image])

    barrier = pltpu.get_barrier_semaphore()

    @pl.loop(1, count)
    def _(step):
        pl.semaphore_signal(
            barrier, inc=1, device_id=place(lax.rem(me + step, count)), device_id_type=MESH
        )

    @pl.loop(0, image_count)
    def _(image):
        raw_copy(image).start()

    maps[me] = unit_map(query_ref[0].astype(jnp.float32)).T.astype(jnp.bfloat16)
    my_info = shortlist_info(shortlist_ref[...], image_count, count)
    infos[me] = my_info
    rank = lax.broadcasted_iota(jnp.int32, (ROWS, LANES), 0)
    spot = lax.broadcasted_iota(jnp.int32, (ROWS, LANES), 1)
    own = jnp.zeros((ROWS, LANES), jnp.int32)
    for k in range(width):
        hit = (my_info[0:1, :] == me) & (my_info[2:3, :] == k)
        slot = jnp.sum(jnp.where(hit, my_info[1:2, :], 0), axis=1, keepdims=True)
        own = jnp.where(spot == k, slot, own)
    own_rows[...] = own
    own_smem = pltpu.make_async_copy(own_rows, own_table, own_sem)
    own_smem.start()
    fill_filters(query_taps, db_taps, filter_query, filter_db)
    peaks[...] = jnp.zeros_like(peaks)
    first_half = image_count // 2

    def normalize(image):
        raw_copy(image).wait()
        units[image] = unit_map(raw[image].astype(jnp.float32)).astype(jnp.bfloat16)

    pl.loop(0, first_half)(normalize)
    pl.semaphore_wait(barrier, count - 1)

    plane_base = pb_count
    partner_base = pb_count + pb_count * chips

    for step in range(1, pb_count):
        map_copy(me, maps.at[me], step, (db, lax.rem(pb + step, pb_count))).start()
    for step in range(1, chips):
        map_copy(
            me, maps.at[me], plane_base + step, (lax.rem(chip + step, chips) * 2 + core, pb)
        ).start()

    @pl.loop(1, count)
    def _(step):
        info_copy(lax.rem(me + step, count), me).start()

    map_copy(me, maps.at[me], partner_base, (chip * 2 + 1 - core, pb)).start()

    pl.loop(first_half, image_count)(normalize)
    own_smem.wait()

    def fill_slots():
        @pl.loop(1, count)
        def _(step):
            info_copy(lax.rem(me + step, count), lax.rem(me + step, count)).wait_recv()

        shard_of = infos[:, 0, :]
        slot_of = infos[:, 1, :]
        bucket_of = infos[:, 2, :]
        lane = lax.broadcasted_iota(jnp.int32, (count, LANES), 1)
        table = jnp.zeros((count, LANES), jnp.int32)
        for k in range(width):
            hit = (shard_of == me) & (bucket_of == k)
            slot = jnp.sum(jnp.where(hit, slot_of, 0), axis=1, keepdims=True)
            table = jnp.where(lane == k, slot, table)
        slot_rows[...] = table
        to_smem = pltpu.make_async_copy(slot_rows, slot_table, local_sem)
        to_smem.start()
        to_smem.wait()

    @pl.loop(0, count)
    def _(turn):
        place_in = turn + (turn + count - 1) // count - (count - 1) * ((turn + 1) // count)
        step = place_in // 2
        half = lax.rem(place_in, 2)
        hop = lax.rem(step, chips)
        other_pb = lax.rem(pb + step // chips, pb_count)
        other_chip = lax.rem(chip + hop, chips)
        source = index_of(other_pb, other_chip, lax.rem(core + half, 2))

        @pl.when((half == 0) & (step >= 1) & (step < pb_count))
        def _():
            line_pb = lax.rem(pb + step, pb_count)
            line = index_of(line_pb, chip, core)
            map_copy(line, maps.at[line], 0, (db, line_pb)).wait_recv()
            for d in range(1, chips):
                map_copy(
                    line,
                    maps.at[line],
                    plane_base + step * chips + d,
                    (lax.rem(chip + d, chips) * 2 + core, pb),
                ).start()

        @pl.when((half == 1) | (hop != 0))
        def _():
            map_copy(source, maps.at[source], 0, (chip * 2 + 1 - core, pb)).wait_recv()

        @pl.when((half == 0) & (step != 0))
        def _():
            map_copy(
                source, maps.at[source], partner_base + step, (chip * 2 + 1 - core, pb)
            ).start()

        @pl.when(turn == 0)
        def _():
            for k in range(width):
                current[k] = own_table[0, k]

        @pl.when(turn == 1)
        def _():
            fill_slots()

        @pl.when(turn != 0)
        def _():
            for k in range(width):
                current[k] = slot_table[source, k]

        for k in range(width):
            slot = current[k]
            correlation = jnp.dot(
                maps[source], units[slot], preferred_element_type=jnp.float32
            )
            positive[k] = jnp.maximum(correlation, 0.0).astype(jnp.bfloat16)
        for k in range(width):
            rectified = positive[k]
            filtered = jnp.dot(
                filter_query[...], rectified, preferred_element_type=jnp.float32
            ) + jnp.dot(rectified, filter_db[...], preferred_element_type=jnp.float32)
            peaks[k : k + 1, :] = jnp.max(filtered, axis=0, keepdims=True)
        best = peaks[...]
        total = jnp.sum(best, axis=1, keepdims=True) * (score_scale / best.shape[1])
        found[source] = jnp.broadcast_to(total, (ROWS, LANES))

        @pl.when(source != me)
        def _():
            back_copy(source, me).start()

    returned[me] = found[me]

    @pl.loop(1, count)
    def _(step):
        other = lax.rem(me + step, count)
        back_copy(other, other).wait_recv()

    my_shard = my_info[0:1, :]
    my_bucket = my_info[2:3, :]
    scores = jnp.zeros((ROWS, LANES), jnp.float32)
    for s in range(count):
        scores = scores + jnp.where((my_shard == s) & (my_bucket == rank), returned[s], 0.0)
    final = jnp.sum(scores, axis=0, keepdims=True)
    out_ref[...] = final
    sorted_ref[...] = descending(final)

    @pl.loop(1, count)
    def _(step):
        other = lax.rem(me + step, count)
        info_copy(other, me).wait_send()
        back_copy(other, me).wait_send()

    for step in range(1, pb_count):
        map_copy(me, maps.at[me], step, (db, pb)).wait_send()
    for step in range(pb_count):
        for d in range(1, chips):
            map_copy(me, maps.at[me], plane_base + step * chips + d, (db, pb)).wait_send()

    @pl.loop(0, pb_count * chips)
    def _(step):
        map_copy(me, maps.at[me], partner_base + step, (db, pb)).wait_send()


def body(db_count, pb_count, query_maps, database, shortlist, kernel_query, kernel_db):
    count = db_count * pb_count
    chips = db_count // 2
    image_count, channels, cells = database.shape
    entries = shortlist.shape[1]
    width = 2 * entries // count
    vmem = pl.BlockSpec(memory_space=pltpu.VMEM)
    row = jax.ShapeDtypeStruct((1, entries), jnp.float32)
    scores, ordered = pl.pallas_call(
        functools.partial(kernel, db_count, pb_count, width),
        out_shape=(row, row),
        in_specs=[vmem, vmem, pl.BlockSpec(memory_space=pl.ANY), vmem, vmem],
        out_specs=(vmem, vmem),
        scratch_shapes=[
            pltpu.VMEM((cells, cells), jnp.bfloat16),
            pltpu.VMEM((cells, cells), jnp.bfloat16),
            pltpu.VMEM((image_count, channels, cells), jnp.bfloat16),
            pltpu.VMEM((width, cells, cells), jnp.bfloat16),
            pltpu.VMEM((count, cells, channels), jnp.bfloat16),
            pltpu.VMEM((count, ROWS, LANES), jnp.int32),
            pltpu.VMEM((image_count, channels, cells), jnp.bfloat16),
            pltpu.VMEM((count, LANES), jnp.int32),
            pltpu.SMEM((count, LANES), jnp.int32),
            pltpu.VMEM((ROWS, LANES), jnp.int32),
            pltpu.SMEM((ROWS, LANES), jnp.int32),
            pltpu.SMEM((width,), jnp.int32),
            pltpu.VMEM((ROWS, cells), jnp.float32),
            pltpu.VMEM((count, ROWS, LANES), jnp.float32),
            pltpu.VMEM((count, ROWS, LANES), jnp.float32),
            pltpu.SemaphoreType.DMA((pb_count + 2 * pb_count * chips,)),
            pltpu.SemaphoreType.DMA((count,)),
            pltpu.SemaphoreType.DMA((count,)),
            pltpu.SemaphoreType.DMA((count,)),
            pltpu.SemaphoreType.DMA((count,)),
            pltpu.SemaphoreType.DMA((count,)),
            pltpu.SemaphoreType.DMA,
            pltpu.SemaphoreType.DMA,
            pltpu.SemaphoreType.DMA((image_count,)),
        ],
        compiler_params=pltpu.CompilerParams(
            collective_id=0, has_side_effects=True, vmem_limit_bytes=56 * 1024 * 1024
        ),
    )(query_maps, shortlist, database, kernel_query, kernel_db)
    return (scores, ordered[:, :TOPK])


def solution(mesh):
    in_specs = (
        P(("db", "pb"), None, None),
        P(("db", "pb"), None, None),
        P(("db", "pb"), None),
        P(),
        P(),
    )
    out_specs = (P(("db", "pb"), None), P(("db", "pb"), None))
    step = functools.partial(body, mesh.shape["db"], mesh.shape["pb"])
    return jax.shard_map(step, mesh=mesh, in_specs=in_specs, out_specs=out_specs, check_vma=False)
```

```python
import functools

import jax
import jax.numpy as jnp
from jax import lax
from jax.experimental import pallas as pl
from jax.experimental.pallas import tpu as pltpu
from jax.sharding import PartitionSpec as P

GRID = 16
TOPK = 100
LANES = 128
ROWS = 8
MESH = pl.DeviceIdType.MESH

epsilon = 1e-06
score_scale = 8.0


def unit_map(values):
    squares = jnp.sum(values * values, axis=0, keepdims=True)
    return values * lax.rsqrt(squares + epsilon)


def fill_filters(query_taps, db_taps, filter_query, filter_db):
    cells = filter_query.shape[0]
    row = lax.broadcasted_iota(jnp.int32, (cells, cells), 0)
    col = lax.broadcasted_iota(jnp.int32, (cells, cells), 1)
    down = (col >> 4) - (row >> 4)
    across = (col & (GRID - 1)) - (row & (GRID - 1))
    near = (jnp.abs(down) <= 1) & (jnp.abs(across) <= 1)
    tap = jnp.where(near, down * 3 + across + 4, -1)
    query_matrix = jnp.zeros((cells, cells), jnp.float32)
    db_matrix = jnp.zeros((cells, cells), jnp.float32)
    query_values = query_taps[...].astype(jnp.float32)
    db_values = db_taps[...].astype(jnp.float32)
    for i in range(3):
        for j in range(3):
            hit = tap == 3 * i + j
            back = tap == 8 - (3 * i + j)
            query_matrix = jnp.where(hit, query_values[i : i + 1, j : j + 1], query_matrix)
            db_matrix = jnp.where(back, db_values[i : i + 1, j : j + 1], db_matrix)
    filter_query[...] = query_matrix.astype(jnp.bfloat16)
    filter_db[...] = db_matrix.astype(jnp.bfloat16)


def shortlist_info(ids, image_count, count):
    entries = ids.shape[1]
    shard = jnp.zeros_like(ids)
    for s in range(1, count):
        shard = shard + jnp.where(ids >= s * image_count, 1, 0)
    slot = ids - shard * image_count
    across = jnp.broadcast_to(shard, (entries, entries))
    above = lax.broadcasted_iota(jnp.int32, (entries, entries), 0)
    beside = lax.broadcasted_iota(jnp.int32, (entries, entries), 1)
    earlier = (across.T == across) & (above < beside)
    bucket = jnp.sum(jnp.where(earlier, 1, 0), axis=0, keepdims=True)
    rank = lax.broadcasted_iota(jnp.int32, (ROWS, entries), 0)
    return jnp.where(rank == 0, shard, jnp.where(rank == 1, slot, bucket))


def descending(row):
    entries = row.shape[1]
    across = jnp.broadcast_to(row, (entries, entries))
    down = across.T
    above = lax.broadcasted_iota(jnp.int32, (entries, entries), 0)
    beside = lax.broadcasted_iota(jnp.int32, (entries, entries), 1)
    ahead = (down > across) | ((down == across) & (above < beside))
    rank = jnp.sum(jnp.where(ahead, 1.0, 0.0), axis=0, keepdims=True)
    rank_down = jnp.broadcast_to(rank, (entries, entries)).T
    chosen = jnp.where(rank_down == beside.astype(jnp.float32), down, 0.0)
    return jnp.sum(chosen, axis=0, keepdims=True)


def kernel(
    db_count,
    pb_count,
    width,
    query_ref,
    shortlist_ref,
    database_ref,
    query_taps,
    db_taps,
    out_ref,
    sorted_ref,
    filter_query,
    filter_db,
    raw,
    positive,
    maps,
    infos,
    units,
    slot_rows,
    slot_table,
    own_rows,
    own_table,
    current,
    peaks,
    found,
    returned,
    map_send,
    map_recv,
    info_send,
    info_recv,
    back_send,
    back_recv,
    local_sem,
    own_sem,
    raw_sem,
):
    count = db_count * pb_count
    chips = db_count // 2
    image_count = database_ref.shape[0]
    db = lax.axis_index("db")
    pb = lax.axis_index("pb")
    chip = db // 2
    core = lax.rem(db, 2)
    me = db * pb_count + pb

    def place(index):
        return (index // pb_count, lax.rem(index, pb_count))

    def index_of(other_pb, other_chip, other_core):
        return (other_chip * 2 + other_core) * pb_count + other_pb

    def map_copy(source, block, send_slot, device):
        return pltpu.make_async_remote_copy(
            src_ref=block,
            dst_ref=maps.at[source],
            send_sem=map_send.at[send_slot],
            recv_sem=map_recv.at[source],
            device_id=device,
            device_id_type=MESH,
        )

    def info_copy(other, owner):
        return pltpu.make_async_remote_copy(
            src_ref=infos.at[me],
            dst_ref=infos.at[owner],
            send_sem=info_send.at[other],
            recv_sem=info_recv.at[owner],
            device_id=place(other),
            device_id_type=MESH,
        )

    def back_copy(source, landed):
        return pltpu.make_async_remote_copy(
            src_ref=found.at[source],
            dst_ref=returned.at[landed],
            send_sem=back_send.at[source],
            recv_sem=back_recv.at[landed],
            device_id=place(source),
            device_id_type=MESH,
        )

    def raw_copy(image):
        return pltpu.make_async_copy(database_ref.at[image], raw.at[image], raw_sem.at[image])

    barrier = pltpu.get_barrier_semaphore()

    @pl.loop(1, count)
    def _(step):
        pl.semaphore_signal(
            barrier, inc=1, device_id=place(lax.rem(me + step, count)), device_id_type=MESH
        )

    @pl.loop(0, image_count)
    def _(image):
        raw_copy(image).start()

    maps[me] = unit_map(query_ref[0].astype(jnp.float32)).T.astype(jnp.bfloat16)
    my_info = shortlist_info(shortlist_ref[...], image_count, count)
    infos[me] = my_info
    rank = lax.broadcasted_iota(jnp.int32, (ROWS, LANES), 0)
    spot = lax.broadcasted_iota(jnp.int32, (ROWS, LANES), 1)
    own = jnp.zeros((ROWS, LANES), jnp.int32)
    for k in range(width):
        hit = (my_info[0:1, :] == me) & (my_info[2:3, :] == k)
        slot = jnp.sum(jnp.where(hit, my_info[1:2, :], 0), axis=1, keepdims=True)
        own = jnp.where(spot == k, slot, own)
    own_rows[...] = own
    own_smem = pltpu.make_async_copy(own_rows, own_table, own_sem)
    own_smem.start()
    fill_filters(query_taps, db_taps, filter_query, filter_db)
    peaks[...] = jnp.zeros_like(peaks)
    first_half = image_count // 2

    def normalize(image):
        raw_copy(image).wait()
        units[image] = unit_map(raw[image].astype(jnp.float32)).astype(jnp.bfloat16)

    pl.loop(0, first_half)(normalize)
    pl.semaphore_wait(barrier, count - 1)

    plane_base = pb_count
    partner_base = pb_count + pb_count * chips

    @pl.loop(1, count)
    def _(step):
        info_copy(lax.rem(me + step, count), me).start()

    for step in range(1, pb_count):
        map_copy(me, maps.at[me], step, (db, lax.rem(pb + step, pb_count))).start()
    for step in range(1, chips):
        map_copy(
            me, maps.at[me], plane_base + step, (lax.rem(chip + step, chips) * 2 + core, pb)
        ).start()

    map_copy(me, maps.at[me], partner_base, (chip * 2 + 1 - core, pb)).start()

    pl.loop(first_half, image_count)(normalize)
    own_smem.wait()

    def fill_slots():
        @pl.loop(1, count)
        def _(step):
            info_copy(lax.rem(me + step, count), lax.rem(me + step, count)).wait_recv()

        shard_of = infos[:, 0, :]
        slot_of = infos[:, 1, :]
        bucket_of = infos[:, 2, :]
        lane = lax.broadcasted_iota(jnp.int32, (count, LANES), 1)
        table = jnp.zeros((count, LANES), jnp.int32)
        for k in range(width):
            hit = (shard_of == me) & (bucket_of == k)
            slot = jnp.sum(jnp.where(hit, slot_of, 0), axis=1, keepdims=True)
            table = jnp.where(lane == k, slot, table)
        slot_rows[...] = table
        to_smem = pltpu.make_async_copy(slot_rows, slot_table, local_sem)
        to_smem.start()
        to_smem.wait()

    @pl.loop(0, count)
    def _(turn):
        place_in = turn + (turn + count - 1) // count - (count - 1) * ((turn + 1) // count)
        step = place_in // 2
        half = lax.rem(place_in, 2)
        hop = lax.rem(step, chips)
        other_pb = lax.rem(pb + step // chips, pb_count)
        other_chip = lax.rem(chip + hop, chips)
        source = index_of(other_pb, other_chip, lax.rem(core + half, 2))

        @pl.when((half == 0) & (step >= 1) & (step < pb_count))
        def _():
            line_pb = lax.rem(pb + step, pb_count)
            line = index_of(line_pb, chip, core)
            map_copy(line, maps.at[line], 0, (db, line_pb)).wait_recv()
            for d in range(1, chips):
                map_copy(
                    line,
                    maps.at[line],
                    plane_base + step * chips + d,
                    (lax.rem(chip + d, chips) * 2 + core, pb),
                ).start()

        @pl.when((half == 1) | (hop != 0))
        def _():
            map_copy(source, maps.at[source], 0, (chip * 2 + 1 - core, pb)).wait_recv()

        @pl.when((half == 0) & (step != 0))
        def _():
            map_copy(
                source, maps.at[source], partner_base + step, (chip * 2 + 1 - core, pb)
            ).start()

        @pl.when(turn == 0)
        def _():
            for k in range(width):
                current[k] = own_table[0, k]

        @pl.when(turn == 1)
        def _():
            fill_slots()

        @pl.when(turn != 0)
        def _():
            for k in range(width):
                current[k] = slot_table[source, k]

        for k in range(width):
            slot = current[k]
            correlation = jnp.dot(
                maps[source], units[slot], preferred_element_type=jnp.float32
            )
            positive[k] = jnp.maximum(correlation, 0.0).astype(jnp.bfloat16)
        for k in range(width):
            rectified = positive[k]
            filtered = jnp.dot(
                filter_query[...], rectified, preferred_element_type=jnp.float32
            ) + jnp.dot(rectified, filter_db[...], preferred_element_type=jnp.float32)
            peaks[k : k + 1, :] = jnp.max(filtered, axis=0, keepdims=True)
        best = peaks[...]
        total = jnp.sum(best, axis=1, keepdims=True) * (score_scale / best.shape[1])
        found[source] = jnp.broadcast_to(total, (ROWS, LANES))

        @pl.when(source != me)
        def _():
            back_copy(source, me).start()

    returned[me] = found[me]

    @pl.loop(1, count)
    def _(step):
        other = lax.rem(me + step, count)
        back_copy(other, other).wait_recv()

    my_shard = my_info[0:1, :]
    my_bucket = my_info[2:3, :]
    scores = jnp.zeros((ROWS, LANES), jnp.float32)
    for s in range(count):
        scores = scores + jnp.where((my_shard == s) & (my_bucket == rank), returned[s], 0.0)
    final = jnp.sum(scores, axis=0, keepdims=True)
    out_ref[...] = final
    sorted_ref[...] = descending(final)

    @pl.loop(1, count)
    def _(step):
        other = lax.rem(me + step, count)
        info_copy(other, me).wait_send()
        back_copy(other, me).wait_send()

    for step in range(1, pb_count):
        map_copy(me, maps.at[me], step, (db, pb)).wait_send()
    for step in range(pb_count):
        for d in range(1, chips):
            map_copy(me, maps.at[me], plane_base + step * chips + d, (db, pb)).wait_send()

    @pl.loop(0, pb_count * chips)
    def _(step):
        map_copy(me, maps.at[me], partner_base + step, (db, pb)).wait_send()


def body(db_count, pb_count, query_maps, database, shortlist, kernel_query, kernel_db):
    count = db_count * pb_count
    chips = db_count // 2
    image_count, channels, cells = database.shape
    entries = shortlist.shape[1]
    width = 2 * entries // count
    vmem = pl.BlockSpec(memory_space=pltpu.VMEM)
    row = jax.ShapeDtypeStruct((1, entries), jnp.float32)
    scores, ordered = pl.pallas_call(
        functools.partial(kernel, db_count, pb_count, width),
        out_shape=(row, row),
        in_specs=[vmem, vmem, pl.BlockSpec(memory_space=pl.ANY), vmem, vmem],
        out_specs=(vmem, vmem),
        scratch_shapes=[
            pltpu.VMEM((cells, cells), jnp.bfloat16),
            pltpu.VMEM((cells, cells), jnp.bfloat16),
            pltpu.VMEM((image_count, channels, cells), jnp.bfloat16),
            pltpu.VMEM((width, cells, cells), jnp.bfloat16),
            pltpu.VMEM((count, cells, channels), jnp.bfloat16),
            pltpu.VMEM((count, ROWS, LANES), jnp.int32),
            pltpu.VMEM((image_count, channels, cells), jnp.bfloat16),
            pltpu.VMEM((count, LANES), jnp.int32),
            pltpu.SMEM((count, LANES), jnp.int32),
            pltpu.VMEM((ROWS, LANES), jnp.int32),
            pltpu.SMEM((ROWS, LANES), jnp.int32),
            pltpu.SMEM((width,), jnp.int32),
            pltpu.VMEM((ROWS, cells), jnp.float32),
            pltpu.VMEM((count, ROWS, LANES), jnp.float32),
            pltpu.VMEM((count, ROWS, LANES), jnp.float32),
            pltpu.SemaphoreType.DMA((pb_count + 2 * pb_count * chips,)),
            pltpu.SemaphoreType.DMA((count,)),
            pltpu.SemaphoreType.DMA((count,)),
            pltpu.SemaphoreType.DMA((count,)),
            pltpu.SemaphoreType.DMA((count,)),
            pltpu.SemaphoreType.DMA((count,)),
            pltpu.SemaphoreType.DMA,
            pltpu.SemaphoreType.DMA,
            pltpu.SemaphoreType.DMA((image_count,)),
        ],
        compiler_params=pltpu.CompilerParams(
            collective_id=0, has_side_effects=True, vmem_limit_bytes=56 * 1024 * 1024
        ),
    )(query_maps, shortlist, database, kernel_query, kernel_db)
    return (scores, ordered[:, :TOPK])


def solution(mesh):
    in_specs = (
        P(("db", "pb"), None, None),
        P(("db", "pb"), None, None),
        P(("db", "pb"), None),
        P(),
        P(),
    )
    out_specs = (P(("db", "pb"), None), P(("db", "pb"), None))
    step = functools.partial(body, mesh.shape["db"], mesh.shape["pb"])
    return jax.shard_map(step, mesh=mesh, in_specs=in_specs, out_specs=out_specs, check_vma=False)
```

```python
import functools

import jax
import jax.numpy as jnp
from jax import lax
from jax.experimental import pallas as pl
from jax.experimental.pallas import tpu as pltpu
from jax.sharding import PartitionSpec as P

GRID = 16
TOPK = 100
LANES = 128
ROWS = 8
MESH = pl.DeviceIdType.MESH

epsilon = 1e-06
score_scale = 8.0


def unit_map(values):
    squares = jnp.sum(values * values, axis=0, keepdims=True)
    return values * lax.rsqrt(squares + epsilon)


def fill_filters(query_taps, db_taps, filter_query, filter_db):
    cells = filter_query.shape[0]
    row = lax.broadcasted_iota(jnp.int32, (cells, cells), 0)
    col = lax.broadcasted_iota(jnp.int32, (cells, cells), 1)
    down = (col >> 4) - (row >> 4)
    across = (col & (GRID - 1)) - (row & (GRID - 1))
    near = (jnp.abs(down) <= 1) & (jnp.abs(across) <= 1)
    tap = jnp.where(near, down * 3 + across + 4, -1)
    query_matrix = jnp.zeros((cells, cells), jnp.float32)
    db_matrix = jnp.zeros((cells, cells), jnp.float32)
    query_values = query_taps[...].astype(jnp.float32)
    db_values = db_taps[...].astype(jnp.float32)
    for i in range(3):
        for j in range(3):
            hit = tap == 3 * i + j
            back = tap == 8 - (3 * i + j)
            query_matrix = jnp.where(hit, query_values[i : i + 1, j : j + 1], query_matrix)
            db_matrix = jnp.where(back, db_values[i : i + 1, j : j + 1], db_matrix)
    filter_query[...] = query_matrix.astype(jnp.bfloat16)
    filter_db[...] = db_matrix.astype(jnp.bfloat16)


def shortlist_info(ids, image_count, count):
    entries = ids.shape[1]
    shard = jnp.zeros_like(ids)
    for s in range(1, count):
        shard = shard + jnp.where(ids >= s * image_count, 1, 0)
    slot = ids - shard * image_count
    across = jnp.broadcast_to(shard, (entries, entries))
    above = lax.broadcasted_iota(jnp.int32, (entries, entries), 0)
    beside = lax.broadcasted_iota(jnp.int32, (entries, entries), 1)
    earlier = (across.T == across) & (above < beside)
    bucket = jnp.sum(jnp.where(earlier, 1, 0), axis=0, keepdims=True)
    rank = lax.broadcasted_iota(jnp.int32, (ROWS, entries), 0)
    return jnp.where(rank == 0, shard, jnp.where(rank == 1, slot, bucket))


def descending(row):
    entries = row.shape[1]
    across = jnp.broadcast_to(row, (entries, entries))
    down = across.T
    above = lax.broadcasted_iota(jnp.int32, (entries, entries), 0)
    beside = lax.broadcasted_iota(jnp.int32, (entries, entries), 1)
    ahead = (down > across) | ((down == across) & (above < beside))
    rank = jnp.sum(jnp.where(ahead, 1.0, 0.0), axis=0, keepdims=True)
    rank_down = jnp.broadcast_to(rank, (entries, entries)).T
    chosen = jnp.where(rank_down == beside.astype(jnp.float32), down, 0.0)
    return jnp.sum(chosen, axis=0, keepdims=True)


def kernel(
    db_count,
    pb_count,
    width,
    query_ref,
    shortlist_ref,
    database_ref,
    query_taps,
    db_taps,
    out_ref,
    sorted_ref,
    filter_query,
    filter_db,
    raw,
    positive,
    maps,
    infos,
    units,
    slot_rows,
    slot_table,
    own_rows,
    own_table,
    current,
    peaks,
    found,
    returned,
    map_send,
    map_recv,
    info_send,
    info_recv,
    back_send,
    back_recv,
    local_sem,
    own_sem,
    raw_sem,
):
    count = db_count * pb_count
    chips = db_count // 2
    image_count = database_ref.shape[0]
    db = lax.axis_index("db")
    pb = lax.axis_index("pb")
    chip = db // 2
    core = lax.rem(db, 2)
    me = db * pb_count + pb

    def place(index):
        return (index // pb_count, lax.rem(index, pb_count))

    def index_of(other_pb, other_chip, other_core):
        return (other_chip * 2 + other_core) * pb_count + other_pb

    def map_copy(source, block, send_slot, device):
        return pltpu.make_async_remote_copy(
            src_ref=block,
            dst_ref=maps.at[source],
            send_sem=map_send.at[send_slot],
            recv_sem=map_recv.at[source],
            device_id=device,
            device_id_type=MESH,
        )

    def info_copy(other, owner):
        return pltpu.make_async_remote_copy(
            src_ref=infos.at[me],
            dst_ref=infos.at[owner],
            send_sem=info_send.at[other],
            recv_sem=info_recv.at[owner],
            device_id=place(other),
            device_id_type=MESH,
        )

    def back_copy(source, landed):
        return pltpu.make_async_remote_copy(
            src_ref=found.at[source],
            dst_ref=returned.at[landed],
            send_sem=back_send.at[source],
            recv_sem=back_recv.at[landed],
            device_id=place(source),
            device_id_type=MESH,
        )

    def raw_copy(image):
        return pltpu.make_async_copy(database_ref.at[image], raw.at[image], raw_sem.at[image])

    barrier = pltpu.get_barrier_semaphore()

    @pl.loop(1, count)
    def _(step):
        pl.semaphore_signal(
            barrier, inc=1, device_id=place(lax.rem(me + step, count)), device_id_type=MESH
        )

    @pl.loop(0, image_count)
    def _(image):
        raw_copy(image).start()

    maps[me] = unit_map(query_ref[0].astype(jnp.float32)).T.astype(jnp.bfloat16)
    my_info = shortlist_info(shortlist_ref[...], image_count, count)
    infos[me] = my_info
    rank = lax.broadcasted_iota(jnp.int32, (ROWS, LANES), 0)
    spot = lax.broadcasted_iota(jnp.int32, (ROWS, LANES), 1)
    own = jnp.zeros((ROWS, LANES), jnp.int32)
    for k in range(width):
        hit = (my_info[0:1, :] == me) & (my_info[2:3, :] == k)
        slot = jnp.sum(jnp.where(hit, my_info[1:2, :], 0), axis=1, keepdims=True)
        own = jnp.where(spot == k, slot, own)
    own_rows[...] = own
    own_smem = pltpu.make_async_copy(own_rows, own_table, own_sem)
    own_smem.start()
    peaks[...] = jnp.zeros_like(peaks)

    def normalize(image):
        raw_copy(image).wait()
        units[image] = unit_map(raw[image].astype(jnp.float32)).astype(jnp.bfloat16)

    pl.semaphore_wait(barrier, count - 1)

    plane_base = pb_count
    partner_base = pb_count + pb_count * chips

    @pl.loop(1, count)
    def _(step):
        info_copy(lax.rem(me + step, count), me).start()

    for step in range(1, pb_count):
        map_copy(me, maps.at[me], step, (db, lax.rem(pb + step, pb_count))).start()
    for step in range(1, chips):
        map_copy(
            me, maps.at[me], plane_base + step, (lax.rem(chip + step, chips) * 2 + core, pb)
        ).start()

    map_copy(me, maps.at[me], partner_base, (chip * 2 + 1 - core, pb)).start()

    fill_filters(query_taps, db_taps, filter_query, filter_db)
    pl.loop(0, image_count)(normalize)
    own_smem.wait()

    def fill_slots():
        @pl.loop(1, count)
        def _(step):
            info_copy(lax.rem(me + step, count), lax.rem(me + step, count)).wait_recv()

        shard_of = infos[:, 0, :]
        slot_of = infos[:, 1, :]
        bucket_of = infos[:, 2, :]
        lane = lax.broadcasted_iota(jnp.int32, (count, LANES), 1)
        table = jnp.zeros((count, LANES), jnp.int32)
        for k in range(width):
            hit = (shard_of == me) & (bucket_of == k)
            slot = jnp.sum(jnp.where(hit, slot_of, 0), axis=1, keepdims=True)
            table = jnp.where(lane == k, slot, table)
        slot_rows[...] = table
        to_smem = pltpu.make_async_copy(slot_rows, slot_table, local_sem)
        to_smem.start()
        to_smem.wait()

    @pl.loop(0, count)
    def _(turn):
        place_in = turn + (turn + count - 1) // count - (count - 1) * ((turn + 1) // count)
        step = place_in // 2
        half = lax.rem(place_in, 2)
        hop = lax.rem(step, chips)
        other_pb = lax.rem(pb + step // chips, pb_count)
        other_chip = lax.rem(chip + hop, chips)
        source = index_of(other_pb, other_chip, lax.rem(core + half, 2))

        @pl.when((half == 0) & (step >= 1) & (step < pb_count))
        def _():
            line_pb = lax.rem(pb + step, pb_count)
            line = index_of(line_pb, chip, core)
            map_copy(line, maps.at[line], 0, (db, line_pb)).wait_recv()
            for d in range(1, chips):
                map_copy(
                    line,
                    maps.at[line],
                    plane_base + step * chips + d,
                    (lax.rem(chip + d, chips) * 2 + core, pb),
                ).start()

        @pl.when((half == 1) | (hop != 0))
        def _():
            map_copy(source, maps.at[source], 0, (chip * 2 + 1 - core, pb)).wait_recv()

        @pl.when((half == 0) & (step != 0))
        def _():
            map_copy(
                source, maps.at[source], partner_base + step, (chip * 2 + 1 - core, pb)
            ).start()

        @pl.when(turn == 0)
        def _():
            for k in range(width):
                current[k] = own_table[0, k]

        @pl.when(turn == 1)
        def _():
            fill_slots()

        @pl.when(turn != 0)
        def _():
            for k in range(width):
                current[k] = slot_table[source, k]

        for k in range(width):
            slot = current[k]
            correlation = jnp.dot(
                maps[source], units[slot], preferred_element_type=jnp.float32
            )
            positive[k] = jnp.maximum(correlation, 0.0).astype(jnp.bfloat16)
        for k in range(width):
            rectified = positive[k]
            filtered = jnp.dot(
                filter_query[...], rectified, preferred_element_type=jnp.float32
            ) + jnp.dot(rectified, filter_db[...], preferred_element_type=jnp.float32)
            peaks[k : k + 1, :] = jnp.max(filtered, axis=0, keepdims=True)
        best = peaks[...]
        total = jnp.sum(best, axis=1, keepdims=True) * (score_scale / best.shape[1])
        found[source] = jnp.broadcast_to(total, (ROWS, LANES))

        @pl.when(source != me)
        def _():
            back_copy(source, me).start()

    returned[me] = found[me]

    @pl.loop(1, count)
    def _(step):
        other = lax.rem(me + step, count)
        back_copy(other, other).wait_recv()

    my_shard = my_info[0:1, :]
    my_bucket = my_info[2:3, :]
    scores = jnp.zeros((ROWS, LANES), jnp.float32)
    for s in range(count):
        scores = scores + jnp.where((my_shard == s) & (my_bucket == rank), returned[s], 0.0)
    final = jnp.sum(scores, axis=0, keepdims=True)
    out_ref[...] = final
    sorted_ref[...] = descending(final)

    @pl.loop(1, count)
    def _(step):
        other = lax.rem(me + step, count)
        info_copy(other, me).wait_send()
        back_copy(other, me).wait_send()

    for step in range(1, pb_count):
        map_copy(me, maps.at[me], step, (db, pb)).wait_send()
    for step in range(pb_count):
        for d in range(1, chips):
            map_copy(me, maps.at[me], plane_base + step * chips + d, (db, pb)).wait_send()

    @pl.loop(0, pb_count * chips)
    def _(step):
        map_copy(me, maps.at[me], partner_base + step, (db, pb)).wait_send()


def body(db_count, pb_count, query_maps, database, shortlist, kernel_query, kernel_db):
    count = db_count * pb_count
    chips = db_count // 2
    image_count, channels, cells = database.shape
    entries = shortlist.shape[1]
    width = 2 * entries // count
    vmem = pl.BlockSpec(memory_space=pltpu.VMEM)
    row = jax.ShapeDtypeStruct((1, entries), jnp.float32)
    scores, ordered = pl.pallas_call(
        functools.partial(kernel, db_count, pb_count, width),
        out_shape=(row, row),
        in_specs=[vmem, vmem, pl.BlockSpec(memory_space=pl.ANY), vmem, vmem],
        out_specs=(vmem, vmem),
        scratch_shapes=[
            pltpu.VMEM((cells, cells), jnp.bfloat16),
            pltpu.VMEM((cells, cells), jnp.bfloat16),
            pltpu.VMEM((image_count, channels, cells), jnp.bfloat16),
            pltpu.VMEM((width, cells, cells), jnp.bfloat16),
            pltpu.VMEM((count, cells, channels), jnp.bfloat16),
            pltpu.VMEM((count, ROWS, LANES), jnp.int32),
            pltpu.VMEM((image_count, channels, cells), jnp.bfloat16),
            pltpu.VMEM((count, LANES), jnp.int32),
            pltpu.SMEM((count, LANES), jnp.int32),
            pltpu.VMEM((ROWS, LANES), jnp.int32),
            pltpu.SMEM((ROWS, LANES), jnp.int32),
            pltpu.SMEM((width,), jnp.int32),
            pltpu.VMEM((ROWS, cells), jnp.float32),
            pltpu.VMEM((count, ROWS, LANES), jnp.float32),
            pltpu.VMEM((count, ROWS, LANES), jnp.float32),
            pltpu.SemaphoreType.DMA((pb_count + 2 * pb_count * chips,)),
            pltpu.SemaphoreType.DMA((count,)),
            pltpu.SemaphoreType.DMA((count,)),
            pltpu.SemaphoreType.DMA((count,)),
            pltpu.SemaphoreType.DMA((count,)),
            pltpu.SemaphoreType.DMA((count,)),
            pltpu.SemaphoreType.DMA,
            pltpu.SemaphoreType.DMA,
            pltpu.SemaphoreType.DMA((image_count,)),
        ],
        compiler_params=pltpu.CompilerParams(
            collective_id=0, has_side_effects=True, vmem_limit_bytes=56 * 1024 * 1024
        ),
    )(query_maps, shortlist, database, kernel_query, kernel_db)
    return (scores, ordered[:, :TOPK])


def solution(mesh):
    in_specs = (
        P(("db", "pb"), None, None),
        P(("db", "pb"), None, None),
        P(("db", "pb"), None),
        P(),
        P(),
    )
    out_specs = (P(("db", "pb"), None), P(("db", "pb"), None))
    step = functools.partial(body, mesh.shape["db"], mesh.shape["pb"])
    return jax.shard_map(step, mesh=mesh, in_specs=in_specs, out_specs=out_specs, check_vma=False)
```
